128 devices in a mesh: dp: 2 (over core), tensor: 64 (over x, z, y).
Axes of the slice: x: 4, y: 4, z: 4, core: 2. Of those that a mesh axis runs over, the one named last changes fastest.
Arguments:
- hidden: bfloat16 [2048, 4096], P(('dp', 'tensor')), parts along dimension 0
- norm_gain: float32 [4096], replicated, may hold values from 0.3 to 3
- head_weight: bfloat16 [256512, 4096], P(('dp', 'tensor')), parts along dimension 0
- targets: int32 [2048], P(('dp', 'tensor')), parts along dimension 0, may hold values from 0 to 128255
- lengths: int32 [24], P('dp'), parts along dimension 0, may hold values from 1 to 256, as said below
- offsets: int32 [24], P('dp'), parts along dimension 0, may hold values from 0 to 1023, as said below
- loss_mask: int32 [2048], P(('dp', 'tensor')), parts along dimension 0, may hold values from 0 to 1, as said below
Outputs:
- token_logprob: float32 [2048], P(('dp', 'tensor')), parts along dimension 0
- token_entropy: float32 [2048], P(('dp', 'tensor')), parts along dimension 0
- sequence_score: float32 [24], P('dp'), parts along dimension 0
The draws below stay inside these ranges and needn't reach their ends.
There are 2 independent parts, one for each index of `dp`. The reference program is written for one: setup_inputs(seed, part) draws one part's arguments, and reference() takes and returns one part's arrays. A program takes and returns all parts, laid end to end along the dimension named above; an argument that names none is the same for every part. Nothing has to cross between parts.
Inputs may be any that keep to these rules, and one draw needn't show every extreme that they name: `lengths`: responses lie in order and do not intersection within the 1024 rows; one has length exactly 256. offsets[k] + lengths[k] <= offsets[k+1], and the last response ends within the pack. `loss_mask`: ones only inside responses; the 16 rows of one index of tensor hold at most 10 ones, exactly 10 on some index.
All inputs are finite; a program needn't handle non-finite values.
Results may differ from the reference program's by a relative error of at most 0.0065.
The reference program's roundings to bfloat16 on the way (of `normed`) count: a program that leaves them out, or rounds other values in their place, can miss the bound.
Values may be sent and summed in bfloat16 or wider, within the bound.
No kernel may reach another device: no remote copies, remote signals or barrier semaphores. Data moves between devices by JAX's collectives and lax.ppermute only.
A program may use at most 128 MiB of HBM per device.

```python
import math
import jax
import jax.numpy as jnp
import numpy as np
from jax import lax

D = 4096
VOCAB_DEV = 2004
TOK_DEV = 16
SEQS = 12
LIVE_DEV = 10
TOKENS = 1024
VOCAB = 128256
MAXLEN = 256
N_TENSOR = 64


def draw_hidden(key, part):
    noise_key = jax.random.fold_in(key, 11)
    row_values = jax.random.normal(noise_key, (TOKENS, D), jnp.float32)
    return row_values.astype(jnp.bfloat16)


def draw_head_weight(key, part):
    base_rows = jax.random.normal(jax.random.fold_in(key, 21), (VOCAB, D), jnp.float32) * (3.0 / math.sqrt(D))
    scale_key = jax.random.fold_in(key, 22)
    row_scale = jnp.exp(jax.random.uniform(scale_key, (VOCAB, 1), jnp.float32, math.log(0.5), math.log(2.0)))
    row_values = base_rows * row_scale
    return row_values.astype(jnp.bfloat16)


def draw_layout(key):
    short_lengths = jax.random.randint(jax.random.fold_in(key, 31), (SEQS,), 1, MAXLEN // 4 + 1)
    longest = jax.random.randint(jax.random.fold_in(key, 32), (), 0, SEQS)
    seq_index = jnp.arange(SEQS, dtype=jnp.int32)
    seq_lengths = jnp.where(seq_index == longest, MAXLEN, short_lengths).astype(jnp.int32)
    slack = TOKENS - jnp.sum(seq_lengths)
    shares = jax.random.randint(jax.random.fold_in(key, 33), (SEQS,), 0, 8)
    gap_sizes = slack * shares // (jnp.sum(shares) + 1)
    seq_offsets = (jnp.cumsum(gap_sizes) + jnp.cumsum(seq_lengths) - seq_lengths).astype(jnp.int32)
    positions = jnp.arange(TOKENS, dtype=jnp.int32)
    inside = (positions[None, :] >= seq_offsets[:, None]) & (positions[None, :] < (seq_offsets + seq_lengths)[:, None])
    covered = jnp.any(inside, axis=0)
    in_long = jnp.any(inside & (seq_index == longest)[:, None], axis=0)
    tool_rows = jax.random.randint(jax.random.fold_in(key, 34), (TOKENS,), 0, 8) == 0
    scored = covered & (in_long | jnp.logical_not(tool_rows))
    block_rows = scored.astype(jnp.int32).reshape(TOKENS // TOK_DEV, TOK_DEV)
    live_rank = jnp.cumsum(block_rows, axis=1)
    capped = (block_rows == 1) & (live_rank <= LIVE_DEV)
    return (seq_lengths, seq_offsets, capped.reshape(TOKENS).astype(jnp.int32))


def draw_lengths(key, part):
    return draw_layout(key)[0]


def draw_offsets(key, part):
    return draw_layout(key)[1]


def draw_loss_mask(key, part):
    return draw_layout(key)[2]


def touch_ends(values, key, least, top_value):
    dims = values.shape
    index_at = [jax.random.randint(jax.random.fold_in(key, axis), (), 0, dims[axis]) for axis in range(len(dims))]
    values = values.at[tuple(index_at)].set(least)
    longest = dims.index(max(dims))
    index_at[longest] = (index_at[longest] + 1) % dims[longest]
    return values.at[tuple(index_at)].set(top_value)


def wide_ids(stream_key, shape, amount, lean):
    weights = [min(1 << octave, amount + 1 - (1 << octave)) * (1 << 20) // math.isqrt((1 << octave) ** lean) + 1 for octave in range((amount + 1).bit_length()) if 1 << octave <= amount]
    width = 1 + sum(weights) // (1 << 30)
    grid = np.cumsum(np.array([max(1, weight // width) for weight in weights]))
    pick = jax.random.randint(jax.random.fold_in(stream_key, 1), shape, 0, int(grid[len(weights) - 1]))
    start = jnp.left_shift(1, jnp.searchsorted(jnp.asarray(grid, jnp.int32), pick, side="right").astype(jnp.int32))
    rank = start - 1 + jax.random.randint(jax.random.fold_in(stream_key, 4), shape, 0, 1 << 30) % jnp.minimum(start, amount + 1 - start)
    return jax.random.permutation(jax.random.fold_in(stream_key, 2), amount)[rank].astype(jnp.int32)


def setup_inputs(seed: int = 0, part: int = 0) -> dict:
    key_of = jax.random.split(jax.random.key(seed), 8)
    part_splits = jax.random.split(jax.random.fold_in(key_of[7], part), 8)
    return {
        "hidden": draw_hidden(jax.random.fold_in(jax.random.fold_in(key_of[7], part), 71), part),
        "norm_gain": jnp.clip(jnp.exp(jax.random.uniform(key_of[1], (D,), jnp.float32, math.log(0.3), math.log(3.0))), 0.3, 3.0),
        "head_weight": draw_head_weight(jax.random.fold_in(jax.random.fold_in(key_of[7], part), 71), part),
        "targets": touch_ends(wide_ids(part_splits[3], (TOKENS,), VOCAB, 2), jax.random.fold_in(part_splits[3], 3), 0, VOCAB - 1).astype(jnp.int32),
        "lengths": draw_lengths(jax.random.fold_in(jax.random.fold_in(key_of[7], part), 71), part),
        "offsets": draw_offsets(jax.random.fold_in(jax.random.fold_in(key_of[7], part), 71), part),
        "loss_mask": draw_loss_mask(jax.random.fold_in(jax.random.fold_in(key_of[7], part), 71), part),
    }


epsilon = 1e-05

def combine_stats(earlier, later):
    peak_one, sum_one, spread_one, picked_one = earlier
    peak_two, sum_two, spread_two, picked_two = later
    new_peak = jnp.maximum(peak_one, peak_two)
    weight_early = jnp.exp(peak_one - new_peak)
    weight_late = jnp.exp(peak_two - new_peak)
    new_sum = weight_early * sum_one + weight_late * sum_two
    new_spread = weight_early * (spread_one + (peak_one - new_peak) * sum_one) + weight_late * (spread_two + (peak_two - new_peak) * sum_two)
    return (new_peak, new_sum, new_spread, picked_one + picked_two)

def reference(hidden, norm_gain, head_weight, targets, lengths, offsets, loss_mask):
    values = hidden.astype(jnp.float32)
    meansq = lax.optimization_barrier(jnp.mean(values * values, axis=1, keepdims=True))
    normed = (values * lax.rsqrt(meansq + epsilon) * norm_gain[None, :]).astype(jnp.bfloat16)
    head_blocks = head_weight.reshape(N_TENSOR, VOCAB_DEV, D)

    def vocab_step(running, inputs):
        shard_index, head_block = inputs
        scores = jnp.dot(normed, head_block.T, preferred_element_type=jnp.float32)
        row_peak = lax.optimization_barrier(jnp.max(scores, axis=1))
        centred = scores - row_peak[:, None]
        expo = jnp.exp(centred)
        row_sum = lax.optimization_barrier(jnp.sum(expo, axis=1))
        row_spread = lax.optimization_barrier(jnp.sum(expo * centred, axis=1))
        column = shard_index * VOCAB_DEV + lax.broadcasted_iota(jnp.int32, scores.shape, 1)
        picked = lax.optimization_barrier(jnp.sum(jnp.where(column == targets[:, None], scores, 0.0), axis=1))
        return (combine_stats(running, (row_peak, row_sum, row_spread, picked)), None)
    start_state = (jnp.full((TOKENS,), -1e+30, jnp.float32), jnp.zeros((TOKENS,), jnp.float32), jnp.zeros((TOKENS,), jnp.float32), jnp.zeros((TOKENS,), jnp.float32))
    final_state, unused = lax.scan(vocab_step, start_state, (jnp.arange(N_TENSOR, dtype=jnp.int32), head_blocks))
    row_peak, sum_exp, spread, target_logit = final_state
    mask_float = loss_mask.astype(jnp.float32)
    log_total = jnp.log(sum_exp)
    token_logprob = (target_logit - row_peak - log_total) * mask_float
    token_entropy = (log_total - spread / sum_exp) * mask_float
    positions = jnp.arange(TOKENS, dtype=jnp.int32)
    inside = (positions[None, :] >= offsets[:, None]) & (positions[None, :] < (offsets + lengths)[:, None])
    sequence_score = lax.optimization_barrier(jnp.sum(jnp.where(inside, token_logprob[None, :], 0.0), axis=1)) / lengths.astype(jnp.float32)
    return (token_logprob, token_entropy, sequence_score)
```

```python
import functools

import jax
import jax.numpy as jnp
import numpy as np
from jax import lax
from jax.experimental import pallas as pl
from jax.experimental.pallas import tpu as pltpu
from jax.sharding import PartitionSpec as P

epsilon = 1e-05

D = 4096
WIDE = D + 128
ROWS = 16
LIVE = 10
LINE = 4 * LIVE
ROWS_A = 24
ROWS_B = LINE - ROWS_A
VOCAB_TILE = 512


X, Z, Y = 0, 1, 2


def shifted_pairs(axis, step):
    pairs = []
    for index in range(64):
        coords = [index // 16, (index // 4) % 4, index % 4]
        coords[axis] = (coords[axis] - step) % 4
        pairs.append((index, coords[0] * 16 + coords[1] * 4 + coords[2]))
    return pairs


def from_ahead(value, axis, step):
    return lax.ppermute(value, "tensor", shifted_pairs(axis, step))


def in_order(pieces, own):
    return [lax.select_n((j - own) % 4, *pieces) for j in range(4)]


def prepare_kernel(own_ref, gain_ref, rows0, rows1, rows2, rows3, a_ref, b_ref):
    own = own_ref[0]
    normed, hots = [], []
    for k, ref in enumerate((rows0, rows1, rows2, rows3)):
        values = ref[:, :D].astype(jnp.float32)
        meansq = jnp.mean(values * values, axis=1, keepdims=True)
        scaled = values * lax.rsqrt(meansq + epsilon) * gain_ref[...]
        extra = ref[:, D:]
        normed.append(jnp.concatenate([scaled.astype(jnp.bfloat16), extra], axis=1))
        base = lax.rem(own + k, 4) * LIVE
        slot = extra[:, 0:1].astype(jnp.float32) + base.astype(jnp.float32)
        lane = lax.broadcasted_iota(jnp.int32, (ROWS, LINE), 1).astype(jnp.float32)
        live = extra[:, 5:6].astype(jnp.float32) > 0.5
        hots.append(jnp.where((slot == lane) & live, 1.0, 0.0).astype(jnp.bfloat16))
    hot = jnp.concatenate(hots, axis=0)
    rows = jnp.concatenate(normed, axis=0)
    line = lax.dot_general(
        hot, rows, (((0,), (0,)), ((), ())), preferred_element_type=jnp.float32
    ).astype(jnp.bfloat16)
    a_ref[...] = line[:ROWS_A]
    b_ref[...] = line[ROWS_A:]


def prepare(own, gain, pieces):
    vmem = pl.BlockSpec(memory_space=pltpu.VMEM)
    return pl.pallas_call(
        prepare_kernel,
        name="prepare",
        out_shape=(
            jax.ShapeDtypeStruct((ROWS_A, WIDE), jnp.bfloat16),
            jax.ShapeDtypeStruct((ROWS_B, WIDE), jnp.bfloat16),
        ),
        in_specs=[pl.BlockSpec(memory_space=pltpu.SMEM)] + [vmem] * 5,
        out_specs=(vmem, vmem),
        cost_estimate=pl.CostEstimate(
            flops=2 * 64 * LINE * WIDE, bytes_accessed=104 * WIDE * 2, transcendentals=64
        ),
    )(own, gain, *pieces)


def score_kernel(vocab_rows, n_pieces, start_ref, *refs):
    piece_refs = refs[:n_pieces]
    weight_ref, out_ref, held = refs[n_pieces:]
    step = pl.program_id(0)
    tile = weight_ref.shape[0]
    total = out_ref.shape[1]

    @pl.when(step == 0)
    def _():
        at = 0
        for ref in piece_refs:
            held[at : at + ref.shape[0], :] = ref[...]
            at += ref.shape[0]
        pick = (
            lax.broadcasted_iota(jnp.int32, (8, 128), 0)
            == lax.broadcasted_iota(jnp.int32, (8, 128), 1)
        ).astype(jnp.bfloat16)
        extra = lax.dot_general(
            pick, held[:, D:], (((1,), (1,)), ((), ())), preferred_element_type=jnp.float32
        )
        ids = extra[1:2] * 4096.0 + extra[2:3] * 64.0 + extra[3:4]
        out_ref[0:1, :] = jnp.full((1, total), -1e30, jnp.float32)
        out_ref[1:4, :] = jnp.zeros((3, total), jnp.float32)
        out_ref[4:5, :] = extra[4:5]
        out_ref[5:6, :] = extra[5:6]
        out_ref[6:7, :] = ids
        out_ref[7:8, :] = ids

    scores = lax.dot_general(
        weight_ref[...],
        held[:, :D],
        (((1,), (1,)), ((), ())),
        preferred_element_type=jnp.float32,
    )
    column = step * tile + lax.broadcasted_iota(jnp.int32, (tile, 1), 0)
    inside = column < vocab_rows
    scores = jnp.where(inside, scores, -1e30)
    peak_before = out_ref[0:1, :]
    peak = jnp.maximum(peak_before, jnp.max(scores, axis=0, keepdims=True))
    centred = scores - peak
    expo = jnp.exp(centred)
    here = jnp.where(inside, column + start_ref[0], -1).astype(jnp.float32) == out_ref[6:7, :]
    shift_by = peak_before - peak
    factor = jnp.exp(shift_by)
    sum_before = out_ref[1:2, :]
    out_ref[0:1, :] = peak
    out_ref[1:2, :] = factor * sum_before + jnp.sum(expo, axis=0, keepdims=True)
    out_ref[2:3, :] = factor * (out_ref[2:3, :] + shift_by * sum_before) + jnp.sum(
        expo * centred, axis=0, keepdims=True
    )
    out_ref[3:4, :] += jnp.sum(jnp.where(here, scores, 0.0), axis=0, keepdims=True)


def score(start, pieces, head_weight):
    total = sum(piece.shape[0] for piece in pieces)
    vocab_rows = head_weight.shape[0]
    steps = pl.cdiv(vocab_rows, VOCAB_TILE)
    whole = [pl.BlockSpec(piece.shape, lambda i: (0, 0)) for piece in pieces]
    return pl.pallas_call(
        functools.partial(score_kernel, vocab_rows, len(pieces)),
        name="score",
        grid=(steps,),
        out_shape=jax.ShapeDtypeStruct((8, total), jnp.float32),
        in_specs=[pl.BlockSpec(memory_space=pltpu.SMEM)]
        + whole
        + [pl.BlockSpec((VOCAB_TILE, D), lambda i: (i, 0))],
        out_specs=pl.BlockSpec((8, total), lambda i: (0, 0)),
        scratch_shapes=[pltpu.VMEM((total, WIDE), jnp.bfloat16)],
        cost_estimate=pl.CostEstimate(
            flops=2 * total * vocab_rows * D,
            bytes_accessed=vocab_rows * D * 2 + total * WIDE * 2,
            transcendentals=total * vocab_rows,
        ),
    )(start, *pieces, head_weight)


def combined(stats):
    peaks = [item[0] for item in stats]
    top = jnp.maximum(jnp.maximum(peaks[0], peaks[2]), jnp.maximum(peaks[1], peaks[3]))
    sums, spreads, picks = [], [], []
    for item in stats:
        shift_by = item[0] - top
        factor = jnp.exp(shift_by)
        sums.append(factor * item[1])
        spreads.append(factor * (item[2] + shift_by * item[1]))
        picks.append(item[3])
    added = [(v[0] + v[2]) + (v[1] + v[3]) for v in (sums, spreads, picks)]
    return jnp.stack([top] + added)


def slot_devices():
    device = np.zeros((64 * LIVE,), np.int32)
    for z in range(4):
        for y in range(4):
            for slot in range(LINE):
                at = (
                    z * 4 * ROWS_A + y * ROWS_A + slot
                    if slot < ROWS_A
                    else 16 * ROWS_A + y * 4 * ROWS_B + z * ROWS_B + slot - ROWS_A
                )
                device[at] = (slot // LIVE) * 16 + z * 4 + y
    return device


def local(hidden, norm_gain, head_weight, targets, lengths, offsets, loss_mask):
    me = lax.axis_index("tensor")
    x, z, y = me // 16, (me // 4) % 4, me % 4
    rank = jnp.sum(
        jnp.where(
            lax.broadcasted_iota(jnp.int32, (ROWS, ROWS), 1)
            < lax.broadcasted_iota(jnp.int32, (ROWS, ROWS), 0),
            loss_mask[None, :],
            0,
        ),
        axis=1,
    )
    columns = [
        rank,
        targets // 4096,
        (targets // 64) % 64,
        targets % 64,
        jnp.arange(ROWS, dtype=jnp.int32),
        loss_mask,
    ]
    lane = lax.broadcasted_iota(jnp.int32, (ROWS, 128), 1)
    extra = jnp.zeros((ROWS, 128), jnp.int32)
    for k, column in enumerate(columns):
        extra = jnp.where(lane == k, column[:, None], extra)
    rows = jnp.concatenate([hidden, extra.astype(jnp.bfloat16)], axis=1)
    line = [rows] + [from_ahead(rows, X, k) for k in (1, 2, 3)]
    part_a, part_b = prepare(x[None], norm_gain[None, :], line)
    row_a = [part_a] + [from_ahead(part_a, Y, k) for k in (1, 2, 3)]
    row_b = [part_b] + [from_ahead(part_b, Z, k) for k in (1, 2, 3)]
    own_a = jnp.concatenate(in_order(row_a, y), axis=0)
    own_b = jnp.concatenate(in_order(row_b, z), axis=0)
    up_a, down_a = from_ahead(own_a, Z, 1), from_ahead(own_a, Z, 3)
    up_b, down_b = from_ahead(own_b, Y, 1), from_ahead(own_b, Y, 3)
    half_a, half_b = own_a.shape[0] // 2, own_b.shape[0] // 2
    far_a = [from_ahead(up_a[:half_a], Z, 1), from_ahead(down_a[half_a:], Z, 3)]
    far_b = [from_ahead(up_b[:half_b], Y, 1), from_ahead(down_b[half_b:], Y, 3)]

    start = (me * head_weight.shape[0])[None]
    near = score(start, [own_a, own_b], head_weight)
    side = score(start, [up_a, down_a, up_b, down_b], head_weight)
    far = score(start, far_a + far_b, head_weight)
    na, nb = own_a.shape[0], own_b.shape[0]
    pieces_a = [near[:, :na], side[:, :na], far[:, :na], side[:, na : 2 * na]]
    pieces_b = [
        near[:, na:],
        side[:, 2 * na : 2 * na + nb],
        far[:, na:],
        side[:, 2 * na + nb :],
    ]
    full = jnp.concatenate(in_order(pieces_a, z) + in_order(pieces_b, y), axis=1)
    stats, place, valid = full[:4], full[4], full[5] > 0.5
    for axis in (Y, Z, X):
        stats = combined([stats] + [from_ahead(stats, axis, k) for k in (1, 2, 3)])

    row_peak, sum_exp, spread, target_logit = stats
    log_total = jnp.log(sum_exp)
    logprob = jnp.where(valid, target_logit - row_peak - log_total, 0.0)
    entropy = jnp.where(valid, log_total - spread / sum_exp, 0.0)
    position = jnp.asarray(slot_devices() * ROWS) + place.astype(jnp.int32)
    mine = (position[None, :] == (me * ROWS + jnp.arange(ROWS))[:, None]) & valid[None, :]
    token_logprob = jnp.sum(jnp.where(mine, logprob[None, :], 0.0), axis=1)
    token_entropy = jnp.sum(jnp.where(mine, entropy[None, :], 0.0), axis=1)
    inside = (position[None, :] >= offsets[:, None]) & (
        position[None, :] < (offsets + lengths)[:, None]
    )
    totals = jnp.sum(jnp.where(inside, logprob[None, :], 0.0), axis=1)
    return token_logprob, token_entropy, totals / lengths.astype(jnp.float32)


def solution(mesh):
    return jax.shard_map(
        local,
        mesh=mesh,
        in_specs=(
            P(("dp", "tensor"), None),
            P(),
            P(("dp", "tensor"), None),
            P(("dp", "tensor")),
            P("dp"),
            P("dp"),
            P(("dp", "tensor")),
        ),
        out_specs=(P(("dp", "tensor")), P(("dp", "tensor")), P("dp")),
        check_vma=False,
    )
```

```python
import functools

import jax
import jax.numpy as jnp
import numpy as np
from jax import lax
from jax.experimental import pallas as pl
from jax.experimental.pallas import tpu as pltpu
from jax.sharding import PartitionSpec as P


epsilon = 1e-05

D = 4096
WIDE = D + 128
ROWS = 16
LIVE = 10
LINE = 4 * LIVE
ROWS_A = 24
ROWS_B = LINE - ROWS_A
VOCAB_TILE = 512


X, Z, Y = 0, 1, 2


def shifted_pairs(axis, step):
    pairs = []
    for index in range(64):
        coords = [index // 16, (index // 4) % 4, index % 4]
        coords[axis] = (coords[axis] - step) % 4
        pairs.append((index, coords[0] * 16 + coords[1] * 4 + coords[2]))
    return pairs


def from_ahead(value, axis, step):
    return lax.ppermute(value, "tensor", shifted_pairs(axis, step))


def three_ahead(value, axis):
    return [from_ahead(value, axis, 1), from_ahead(value, axis, 2), from_ahead(value, axis, 3)]


def in_order(pieces, own):
    return [lax.select_n((j - own) % 4, *pieces) for j in range(4)]


def pack_kernel(hidden_ref, targets_ref, mask_ref, out_ref):
    row = lax.broadcasted_iota(jnp.int32, (ROWS, ROWS), 0)
    other = lax.broadcasted_iota(jnp.int32, (ROWS, ROWS), 1)

    def total(chosen, values):
        return jnp.sum(jnp.where(chosen, values, 0), axis=1, keepdims=True)

    target = total(row == other, targets_ref[...])
    columns = [
        total(other < row, mask_ref[...]),
        target >> 12,
        (target >> 6) & 63,
        target & 63,
        row[:, 0:1],
        total(row == other, mask_ref[...]),
    ]
    lane = lax.broadcasted_iota(jnp.int32, (ROWS, 128), 1)
    extra = jnp.zeros((ROWS, 128), jnp.int32)
    for k, column in enumerate(columns):
        extra = jnp.where(lane == k, column, extra)
    out_ref[:, :D] = hidden_ref[...]
    out_ref[:, D:] = extra.astype(jnp.float32).astype(jnp.bfloat16)


def pack(hidden, targets, mask):
    vmem = pl.BlockSpec(memory_space=pltpu.VMEM)
    return pl.pallas_call(
        pack_kernel,
        name="pack",
        out_shape=jax.ShapeDtypeStruct((ROWS, WIDE), jnp.bfloat16),
        in_specs=[vmem] * 3,
        out_specs=vmem,
        cost_estimate=pl.CostEstimate(
            flops=ROWS * WIDE, bytes_accessed=4 * ROWS * WIDE, transcendentals=0
        ),
    )(hidden, targets, mask)


def prepare_kernel(own_ref, gain_ref, rows0, rows1, rows2, rows3, a_ref, b_ref):
    own = own_ref[0]
    normed, hots = [], []
    for k, ref in enumerate((rows0, rows1, rows2, rows3)):
        values = ref[:, :D].astype(jnp.float32)
        meansq = jnp.mean(values * values, axis=1, keepdims=True)
        scaled = values * lax.rsqrt(meansq + epsilon) * gain_ref[...]
        extra = ref[:, D:]
        normed.append(jnp.concatenate([scaled.astype(jnp.bfloat16), extra], axis=1))
        base = lax.rem(own + k, 4) * LIVE
        slot = extra[:, 0:1].astype(jnp.float32) + base.astype(jnp.float32)
        lane = lax.broadcasted_iota(jnp.int32, (ROWS, LINE), 1).astype(jnp.float32)
        live = extra[:, 5:6].astype(jnp.float32) > 0.5
        hots.append(jnp.where((slot == lane) & live, 1.0, 0.0).astype(jnp.bfloat16))
    hot = jnp.concatenate(hots, axis=0)
    rows = jnp.concatenate(normed, axis=0)
    line = lax.dot_general(
        hot, rows, (((0,), (0,)), ((), ())), preferred_element_type=jnp.float32
    ).astype(jnp.bfloat16)
    a_ref[...] = line[:ROWS_A]
    b_ref[...] = line[ROWS_A:]


def prepare(own, gain, pieces):
    vmem = pl.BlockSpec(memory_space=pltpu.VMEM)
    return pl.pallas_call(
        prepare_kernel,
        name="prepare",
        out_shape=(
            jax.ShapeDtypeStruct((ROWS_A, WIDE), jnp.bfloat16),
            jax.ShapeDtypeStruct((ROWS_B, WIDE), jnp.bfloat16),
        ),
        in_specs=[pl.BlockSpec(memory_space=pltpu.SMEM)] + [vmem] * 5,
        out_specs=(vmem, vmem),
        cost_estimate=pl.CostEstimate(
            flops=2 * 64 * LINE * WIDE, bytes_accessed=104 * WIDE * 2, transcendentals=64
        ),
    )(own, gain, *pieces)


def fetch(piece_refs, held, sems):
    copies, at = [], 0
    for k, ref in enumerate(piece_refs):
        rows = ref.shape[0]
        copies.append(pltpu.make_async_copy(ref, held.at[pl.ds(at, rows), :], sems.at[k]))
        at += rows
    for copy in copies:
        copy.start()
    for copy in copies:
        copy.wait()


def accumulate(step, vocab_rows, start, held, weight_ref, acc):
    rows = held.shape[0]

    @pl.when(step == 0)
    def _():
        acc[0] = jnp.full((rows, 128), -1e30, jnp.float32)
        acc[1] = jnp.zeros((rows, 128), jnp.float32)
        acc[2] = jnp.zeros((rows, 128), jnp.float32)
        acc[3] = jnp.zeros((rows, 128), jnp.float32)
        acc[4] = held[:, D:].astype(jnp.float32)

    tile = weight_ref.shape[0]
    scores = lax.dot_general(
        held[:, :D],
        weight_ref[...],
        (((1,), (1,)), ((), ())),
        preferred_element_type=jnp.float32,
    )
    lane = lax.broadcasted_iota(jnp.int32, (1, 128), 1)
    base = step * tile
    groups = [
        jnp.where(base + k + lane < vocab_rows, scores[:, k : k + 128], -1e30)
        for k in range(0, tile, 128)
    ]
    extra = acc[4]
    ids = extra[:, 1:2] * 4096.0 + extra[:, 2:3] * 64.0 + extra[:, 3:4]
    local_id = ids.astype(jnp.int32) - start
    local_id = jnp.where(local_id < vocab_rows, local_id, -1) - base
    before, sum_before = acc[0], acc[1]
    peak = functools.reduce(jnp.maximum, groups, before)
    shift_by = before - peak
    factor = jnp.exp(shift_by)
    total = factor * sum_before
    spread = factor * (acc[2] + shift_by * sum_before)
    picked = acc[3]
    for k, group in enumerate(groups):
        centred = group - peak
        expo = jnp.exp(centred)
        total = total + expo
        spread = spread + expo * centred
        picked = jnp.where(local_id == lane + 128 * k, group, picked)
    acc[0], acc[1], acc[2], acc[3] = peak, total, spread, picked


def near_kernel(vocab_rows, n_pieces, place_ref, *refs):
    weight_ref, acc, held, sems = refs[n_pieces:]
    step = pl.program_id(0)

    @pl.when(step == 0)
    def _():
        fetch(refs[:n_pieces], held, sems)

    accumulate(step, vocab_rows, place_ref[0], held, weight_ref, acc)


def rest_kernel(vocab_rows, n_pieces, na, nb, place_ref, *refs):
    near_ref, weight_ref, out_ref, info_ref, held, acc, all_rows, sems = refs[n_pieces:]
    step = pl.program_id(0)

    @pl.when(step == 0)
    def _():
        fetch(refs[:n_pieces], held, sems)

    accumulate(step, vocab_rows, place_ref[0], held, weight_ref, acc)

    @pl.when(step == pl.num_programs(0) - 1)
    def _():
        z, y = place_ref[1], place_ref[2]
        for k in range(4):
            to_a = pl.multiple_of(lax.rem(z + k, 4) * na, na)
            to_b = pl.multiple_of(4 * na + lax.rem(y + k, 4) * nb, nb)
            if k == 0:
                all_rows[:, pl.ds(to_a, na), :] = near_ref[:, :na, :]
                all_rows[:, pl.ds(to_b, nb), :] = near_ref[:, na:, :]
            else:
                at_a, at_b = (k - 1) * na, 3 * na + (k - 1) * nb
                all_rows[:, pl.ds(to_a, na), :] = acc[:, at_a : at_a + na, :]
                all_rows[:, pl.ds(to_b, nb), :] = acc[:, at_b : at_b + nb, :]
        for at in range(0, all_rows.shape[1], 128):
            peaks, sums, spreads, picks, extra = [
                all_rows[plane, at : at + 128, :].T for plane in range(5)
            ]
            top = jnp.max(peaks, axis=0, keepdims=True)
            shift_by = peaks - top
            factor = jnp.exp(shift_by)
            here = slice(at, at + 128)
            out_ref[0:1, here] = top
            out_ref[1:2, here] = jnp.sum(factor * sums, axis=0, keepdims=True)
            out_ref[2:3, here] = jnp.sum(
                factor * (spreads + shift_by * sums), axis=0, keepdims=True
            )
            out_ref[3:4, here] = jnp.sum(picks, axis=0, keepdims=True)
            info_ref[:, here] = extra[:8]


def score_cost(total, vocab_rows):
    return pl.CostEstimate(
        flops=2 * total * vocab_rows * D,
        bytes_accessed=vocab_rows * D * 2 + total * WIDE * 2,
        transcendentals=total * vocab_rows,
    )


def score_near(place, pieces, head_weight):
    total = sum(piece.shape[0] for piece in pieces)
    vocab_rows = head_weight.shape[0]
    return pl.pallas_call(
        functools.partial(near_kernel, vocab_rows, len(pieces)),
        name="near",
        grid=(pl.cdiv(vocab_rows, VOCAB_TILE),),
        out_shape=jax.ShapeDtypeStruct((5, total, 128), jnp.float32),
        in_specs=[pl.BlockSpec(memory_space=pltpu.SMEM)]
        + [pl.BlockSpec(memory_space=pl.ANY)] * len(pieces)
        + [pl.BlockSpec((VOCAB_TILE, D), lambda i: (i, 0))],
        out_specs=pl.BlockSpec((5, total, 128), lambda i: (0, 0, 0)),
        scratch_shapes=[
            pltpu.VMEM((total, WIDE), jnp.bfloat16),
            pltpu.SemaphoreType.DMA((len(pieces),)),
        ],
        cost_estimate=score_cost(total, vocab_rows),
    )(place, *pieces, head_weight)


def score_rest(place, pieces, near, head_weight, na, nb):
    total = sum(piece.shape[0] for piece in pieces)
    vocab_rows = head_weight.shape[0]
    return pl.pallas_call(
        functools.partial(rest_kernel, vocab_rows, len(pieces), na, nb),
        name="rest",
        grid=(pl.cdiv(vocab_rows, VOCAB_TILE),),
        out_shape=(
            jax.ShapeDtypeStruct((4, total + na + nb), jnp.float32),
            jax.ShapeDtypeStruct((8, total + na + nb), jnp.float32),
        ),
        in_specs=[pl.BlockSpec(memory_space=pltpu.SMEM)]
        + [pl.BlockSpec(memory_space=pl.ANY)] * len(pieces)
        + [pl.BlockSpec(near.shape, lambda i: (0, 0, 0)), pl.BlockSpec((VOCAB_TILE, D), lambda i: (i, 0))],
        out_specs=(
            pl.BlockSpec((4, total + na + nb), lambda i: (0, 0)),
            pl.BlockSpec((8, total + na + nb), lambda i: (0, 0)),
        ),
        scratch_shapes=[
            pltpu.VMEM((total, WIDE), jnp.bfloat16),
            pltpu.VMEM((5, total, 128), jnp.float32),
            pltpu.VMEM((5, total + na + nb, 128), jnp.float32),
            pltpu.SemaphoreType.DMA((len(pieces),)),
        ],
        cost_estimate=score_cost(total, vocab_rows),
    )(place, *pieces, near, head_weight)


def finish_kernel(me_ref, gathered, info, device, offsets, lengths, logprob, entropy, sequence):
    peaks = gathered[:, 0, :]
    sums = gathered[:, 1, :]
    top = jnp.max(peaks, axis=0, keepdims=True)
    shift_by = peaks - top
    factor = jnp.exp(shift_by)
    sum_exp = jnp.sum(factor * sums, axis=0, keepdims=True)
    spread = jnp.sum(factor * (gathered[:, 2, :] + shift_by * sums), axis=0, keepdims=True)
    target_logit = jnp.sum(gathered[:, 3, :], axis=0, keepdims=True)
    log_total = jnp.log(sum_exp)
    valid = info[5:6, :] > 0.5
    row_logprob = jnp.where(valid, target_logit - top - log_total, 0.0)
    row_entropy = jnp.where(valid, log_total - spread / sum_exp, 0.0)
    position = device[...] * ROWS + info[4:5, :].astype(jnp.int32)
    position = jnp.where(valid, position, -1)
    own = me_ref[0] * ROWS + lax.broadcasted_iota(jnp.int32, (ROWS, 1), 0)
    mine = position == own

    def across(column):
        count = column.shape[0]
        row = lax.broadcasted_iota(jnp.int32, (count, count), 0)
        lane = lax.broadcasted_iota(jnp.int32, (count, count), 1)
        return jnp.sum(jnp.where(row == lane, column, 0), axis=0, keepdims=True)

    def down(line):
        count = line.shape[1]
        row = lax.broadcasted_iota(jnp.int32, (count, count), 0)
        lane = lax.broadcasted_iota(jnp.int32, (count, count), 1)
        return jnp.sum(jnp.where(row == lane, line, 0), axis=1, keepdims=True)

    logprob[...] = across(jnp.sum(jnp.where(mine, row_logprob, 0.0), axis=1, keepdims=True))
    entropy[...] = across(jnp.sum(jnp.where(mine, row_entropy, 0.0), axis=1, keepdims=True))
    first = down(offsets[...])
    inside = (position >= first) & (position < first + down(lengths[...]))
    totals = jnp.sum(jnp.where(inside, row_logprob, 0.0), axis=1, keepdims=True)
    sequence[...] = across(totals) / lengths[...].astype(jnp.float32)


def finish(me, gathered, info, offsets, lengths):
    vmem = pl.BlockSpec(memory_space=pltpu.VMEM)
    count = lengths.shape[0]
    return pl.pallas_call(
        finish_kernel,
        name="finish",
        out_shape=(
            jax.ShapeDtypeStruct((1, ROWS), jnp.float32),
            jax.ShapeDtypeStruct((1, ROWS), jnp.float32),
            jax.ShapeDtypeStruct((1, count), jnp.float32),
        ),
        in_specs=[pl.BlockSpec(memory_space=pltpu.SMEM)] + [vmem] * 5,
        out_specs=(vmem, vmem, vmem),
    )(me[None], gathered, info, slot_devices()[None, :], offsets[None, :], lengths[None, :])


def slot_devices():
    device = np.zeros((64 * LIVE,), np.int32)
    for z in range(4):
        for y in range(4):
            for slot in range(LINE):
                at = (
                    z * 4 * ROWS_A + y * ROWS_A + slot
                    if slot < ROWS_A
                    else 16 * ROWS_A + y * 4 * ROWS_B + z * ROWS_B + slot - ROWS_A
                )
                device[at] = (slot // LIVE) * 16 + z * 4 + y
    return device


def local(hidden, norm_gain, head_weight, targets, lengths, offsets, loss_mask):
    me = lax.axis_index("tensor")
    x, z, y = me // 16, (me // 4) % 4, me % 4
    rows = pack(hidden, targets[None, :], loss_mask[None, :])
    line = [rows] + three_ahead(rows, X)
    part_a, part_b = prepare(x[None], norm_gain[None, :], line)
    row_a = [part_a] + three_ahead(part_a, Y)
    row_b = [part_b] + three_ahead(part_b, Z)
    own_a = jnp.concatenate(in_order(row_a, y), axis=0)
    own_b = jnp.concatenate(in_order(row_b, z), axis=0)
    up_a = from_ahead(own_a, Z, 1)
    down_a = from_ahead(own_a, Z, 3)
    up_b = from_ahead(own_b, Y, 1)
    down_b = from_ahead(own_b, Y, 3)
    na, nb = own_a.shape[0], own_b.shape[0]
    far_a = [from_ahead(up_a[: na // 2], Z, 1), from_ahead(down_a[na // 2 :], Z, 3)]
    far_b = [from_ahead(up_b[: nb // 2], Y, 1), from_ahead(down_b[nb // 2 :], Y, 3)]

    place = jnp.stack([me * head_weight.shape[0], z, y])
    near = score_near(place, [own_a, own_b], head_weight)
    stats, info = score_rest(
        place, [up_a, *far_a, down_a, up_b, *far_b, down_b], near, head_weight, na, nb
    )
    copies = jnp.broadcast_to(stats[None], (64,) + stats.shape)
    gathered = lax.all_to_all(copies, "tensor", 0, 0, tiled=True)
    token_logprob, token_entropy, score = finish(me, gathered, info, offsets, lengths)
    return token_logprob[0], token_entropy[0], score[0]


def solution(mesh):
    return jax.shard_map(
        local,
        mesh=mesh,
        in_specs=(
            P(("dp", "tensor"), None),
            P(),
            P(("dp", "tensor"), None),
            P(("dp", "tensor")),
            P("dp"),
            P("dp"),
            P(("dp", "tensor")),
        ),
        out_specs=(P(("dp", "tensor")), P(("dp", "tensor")), P("dp")),
        check_vma=False,
    )
```

```python
import functools

import jax
import jax.numpy as jnp
import numpy as np
from jax import lax
from jax.experimental import pallas as pl
from jax.experimental.pallas import tpu as pltpu
from jax.sharding import PartitionSpec as P


epsilon = 1e-05

D = 4096
WIDE = D + 128
ROWS = 16
LIVE = 10
LINE = 4 * LIVE
ROWS_A = 24
ROWS_B = LINE - ROWS_A
VOCAB_TILE = 512


X, Z, Y = 0, 1, 2


def shifted_pairs(axis, step):
    pairs = []
    for index in range(64):
        coords = [index // 16, (index // 4) % 4, index % 4]
        coords[axis] = (coords[axis] - step) % 4
        pairs.append((index, coords[0] * 16 + coords[1] * 4 + coords[2]))
    return pairs


def from_ahead(value, axis, step):
    return lax.ppermute(value, "tensor", shifted_pairs(axis, step))


def three_ahead(value, axis):
    return [from_ahead(value, axis, 1), from_ahead(value, axis, 2), from_ahead(value, axis, 3)]


def in_vmem(value):
    return pltpu.with_memory_space_constraint(value, pltpu.VMEM)


def pack_kernel(hidden_ref, targets_ref, mask_ref, out_ref):
    row = lax.broadcasted_iota(jnp.int32, (ROWS, ROWS), 0)
    other = lax.broadcasted_iota(jnp.int32, (ROWS, ROWS), 1)

    def total(chosen, values):
        return jnp.sum(jnp.where(chosen, values, 0), axis=1, keepdims=True)

    target = total(row == other, targets_ref[...])
    columns = [
        total(other < row, mask_ref[...]),
        target >> 12,
        (target >> 6) & 63,
        target & 63,
        row[:, 0:1],
        total(row == other, mask_ref[...]),
    ]
    lane = lax.broadcasted_iota(jnp.int32, (ROWS, 128), 1)
    extra = jnp.zeros((ROWS, 128), jnp.int32)
    for k, column in enumerate(columns):
        extra = jnp.where(lane == k, column, extra)
    out_ref[:, :D] = hidden_ref[...]
    out_ref[:, D:] = extra.astype(jnp.float32).astype(jnp.bfloat16)


def pack(hidden, targets, mask):
    vmem = pl.BlockSpec(memory_space=pltpu.VMEM)
    return pl.pallas_call(
        pack_kernel,
        name="pack",
        out_shape=jax.ShapeDtypeStruct((ROWS, WIDE), jnp.bfloat16),
        in_specs=[vmem] * 3,
        out_specs=vmem,
        cost_estimate=pl.CostEstimate(
            flops=ROWS * WIDE, bytes_accessed=4 * ROWS * WIDE, transcendentals=0
        ),
    )(hidden, targets, mask)


def hold_kernel(weight_ref, out_ref, sem):
    copy = pltpu.make_async_copy(weight_ref, out_ref, sem)
    copy.start()
    copy.wait()


def hold(head_weight):
    return pl.pallas_call(
        hold_kernel,
        name="hold",
        out_shape=pltpu.VMEM(head_weight.shape, head_weight.dtype),
        in_specs=[pl.BlockSpec(memory_space=pl.ANY)],
        out_specs=pl.BlockSpec(memory_space=pltpu.VMEM),
        scratch_shapes=[pltpu.SemaphoreType.DMA],
        compiler_params=pltpu.CompilerParams(vmem_limit_bytes=4 * 1024 * 1024),
        cost_estimate=pl.CostEstimate(
            flops=0, bytes_accessed=2 * head_weight.size, transcendentals=0
        ),
    )(pltpu.with_memory_space_constraint(head_weight, pltpu.HBM))


def prepare_kernel(own_ref, gain_ref, rows0, rows1, rows2, rows3, a_ref, b_ref):
    own = own_ref[0]
    normed, hots = [], []
    for k, ref in enumerate((rows0, rows1, rows2, rows3)):
        values = ref[:, :D].astype(jnp.float32)
        meansq = jnp.mean(values * values, axis=1, keepdims=True)
        scaled = values * lax.rsqrt(meansq + epsilon) * gain_ref[...]
        extra = ref[:, D:]
        normed.append(jnp.concatenate([scaled.astype(jnp.bfloat16), extra], axis=1))
        base = lax.rem(own + k, 4) * LIVE
        slot = extra[:, 0:1].astype(jnp.float32) + base.astype(jnp.float32)
        lane = lax.broadcasted_iota(jnp.int32, (ROWS, LINE), 1).astype(jnp.float32)
        live = extra[:, 5:6].astype(jnp.float32) > 0.5
        hots.append(jnp.where((slot == lane) & live, 1.0, 0.0).astype(jnp.bfloat16))
    hot = jnp.concatenate(hots, axis=0)
    rows = jnp.concatenate(normed, axis=0)
    line = lax.dot_general(
        hot, rows, (((0,), (0,)), ((), ())), preferred_element_type=jnp.float32
    ).astype(jnp.bfloat16)
    a_ref[...] = line[:ROWS_A]
    b_ref[...] = line[ROWS_A:]


def prepare(own, gain, pieces):
    vmem = pl.BlockSpec(memory_space=pltpu.VMEM)
    return pl.pallas_call(
        prepare_kernel,
        name="prepare",
        out_shape=(
            jax.ShapeDtypeStruct((ROWS_A, WIDE), jnp.bfloat16),
            jax.ShapeDtypeStruct((ROWS_B, WIDE), jnp.bfloat16),
        ),
        in_specs=[pl.BlockSpec(memory_space=pltpu.SMEM)] + [vmem] * 5,
        out_specs=(vmem, vmem),
        compiler_params=pltpu.CompilerParams(vmem_limit_bytes=8 * 1024 * 1024),
        cost_estimate=pl.CostEstimate(
            flops=2 * 64 * LINE * WIDE, bytes_accessed=104 * WIDE * 2, transcendentals=64
        ),
    )(own, gain, *pieces)


def fetch(piece_refs, held, sems):
    copies, at = [], 0
    for k, ref in enumerate(piece_refs):
        rows = ref.shape[0]
        copies.append(pltpu.make_async_copy(ref, held.at[pl.ds(at, rows), :], sems.at[k]))
        at += rows
    for copy in copies:
        copy.start()
    for copy in copies:
        copy.wait()


def accumulate(step, vocab_rows, start, held, weight_ref, acc):
    rows = held.shape[0]

    @pl.when(step == 0)
    def _():
        acc[0] = jnp.full((rows, 128), -1e30, jnp.float32)
        acc[1] = jnp.zeros((rows, 128), jnp.float32)
        acc[2] = jnp.zeros((rows, 128), jnp.float32)
        acc[3] = jnp.zeros((rows, 128), jnp.float32)
        acc[4] = held[:, D:].astype(jnp.float32)

    tile = weight_ref.shape[0]
    scores = lax.dot_general(
        held[:, :D],
        weight_ref[...],
        (((1,), (1,)), ((), ())),
        preferred_element_type=jnp.float32,
    )
    lane = lax.broadcasted_iota(jnp.int32, (1, 128), 1)
    base = step * tile
    groups = [
        jnp.where(base + k + lane < vocab_rows, scores[:, k : k + 128], -1e30)
        for k in range(0, tile, 128)
    ]
    extra = acc[4]
    ids = extra[:, 1:2] * 4096.0 + extra[:, 2:3] * 64.0 + extra[:, 3:4]
    local_id = ids.astype(jnp.int32) - start
    local_id = jnp.where(local_id < vocab_rows, local_id, -1) - base
    before, sum_before = acc[0], acc[1]
    peak = functools.reduce(jnp.maximum, groups, before)
    shift_by = before - peak
    factor = jnp.exp(shift_by)
    total = factor * sum_before
    spread = factor * (acc[2] + shift_by * sum_before)
    picked = acc[3]
    for k, group in enumerate(groups):
        centred = group - peak
        expo = jnp.exp(centred)
        total = total + expo
        spread = spread + expo * centred
        picked = jnp.where(local_id == lane + 128 * k, group, picked)
    acc[0], acc[1], acc[2], acc[3] = peak, total, spread, picked


def near_kernel(vocab_rows, n_pieces, place_ref, *refs):
    weight_ref, acc, held, sems = refs[n_pieces:]
    step = pl.program_id(0)

    @pl.when(step == 0)
    def _():
        fetch(refs[:n_pieces], held, sems)

    accumulate(step, vocab_rows, place_ref[0], held, weight_ref, acc)


def rest_kernel(vocab_rows, n_pieces, na, nb, place_ref, *refs):
    near_ref, side_ref, weight_ref, out_ref, info_ref, held, acc, all_rows, sems = refs[n_pieces:]
    step = pl.program_id(0)

    @pl.when(step == 0)
    def _():
        fetch(refs[:n_pieces], held, sems)

    accumulate(step, vocab_rows, place_ref[0], held, weight_ref, acc)

    @pl.when(step == pl.num_programs(0) - 1)
    def _():
        z, y = place_ref[1], place_ref[2]
        for k in range(4):
            from_a, at_a = ((near_ref, 0), (side_ref, 0), (acc, 0), (side_ref, na))[k]
            from_b, at_b = (near_ref, na) if k == 0 else (acc, na + (k - 1) * nb)
            for j in range(4):
                to_a = lax.rem(z + k, 4) * na + lax.rem(y + j, 4) * ROWS_A
                to_b = 4 * na + lax.rem(y + k, 4) * nb + lax.rem(z + j, 4) * ROWS_B
                one_a = slice(at_a + j * ROWS_A, at_a + (j + 1) * ROWS_A)
                one_b = slice(at_b + j * ROWS_B, at_b + (j + 1) * ROWS_B)
                into_a = pl.ds(pl.multiple_of(to_a, 8), ROWS_A)
                into_b = pl.ds(pl.multiple_of(to_b, 8), ROWS_B)
                all_rows[:, into_a, :] = from_a[:, one_a, :]
                all_rows[:, into_b, :] = from_b[:, one_b, :]
        for at in range(0, all_rows.shape[1], 128):
            peaks, sums, spreads, picks, extra = [
                all_rows[plane, at : at + 128, :].T for plane in range(5)
            ]
            top = jnp.max(peaks, axis=0, keepdims=True)
            shift_by = peaks - top
            factor = jnp.exp(shift_by)
            here = slice(at, at + 128)
            out_ref[0:1, here] = top
            out_ref[1:2, here] = jnp.sum(factor * sums, axis=0, keepdims=True)
            out_ref[2:3, here] = jnp.sum(
                factor * (spreads + shift_by * sums), axis=0, keepdims=True
            )
            out_ref[3:4, here] = jnp.sum(picks, axis=0, keepdims=True)
            info_ref[:, here] = extra[:8]


def score_params():
    return pltpu.CompilerParams(vmem_limit_bytes=24 * 1024 * 1024)


def score_cost(total, vocab_rows):
    return pl.CostEstimate(
        flops=2 * total * vocab_rows * D,
        bytes_accessed=vocab_rows * D * 2 + total * WIDE * 2,
        transcendentals=total * vocab_rows,
    )


def score_part(place, pieces, head_weight):
    total = sum(piece.shape[0] for piece in pieces)
    vocab_rows = head_weight.shape[0]
    return pl.pallas_call(
        functools.partial(near_kernel, vocab_rows, len(pieces)),
        grid=(pl.cdiv(vocab_rows, VOCAB_TILE),),
        out_shape=jax.ShapeDtypeStruct((5, total, 128), jnp.float32),
        in_specs=[pl.BlockSpec(memory_space=pltpu.SMEM)]
        + [pl.BlockSpec(memory_space=pl.ANY)] * len(pieces)
        + [pl.BlockSpec((VOCAB_TILE, D), lambda i: (i, 0))],
        out_specs=pl.BlockSpec((5, total, 128), lambda i: (0, 0, 0)),
        scratch_shapes=[
            pltpu.VMEM((total, WIDE), jnp.bfloat16),
            pltpu.SemaphoreType.DMA((len(pieces),)),
        ],
        compiler_params=score_params(),
        cost_estimate=score_cost(total, vocab_rows),
    )(place, *pieces, head_weight)


def score_rest(place, pieces, near, side, head_weight, na, nb):
    total = sum(piece.shape[0] for piece in pieces)
    slots = 4 * (na + nb)
    vocab_rows = head_weight.shape[0]
    return pl.pallas_call(
        functools.partial(rest_kernel, vocab_rows, len(pieces), na, nb),
        name="rest",
        grid=(pl.cdiv(vocab_rows, VOCAB_TILE),),
        out_shape=(
            jax.ShapeDtypeStruct((4, slots), jnp.float32),
            jax.ShapeDtypeStruct((8, slots), jnp.float32),
        ),
        in_specs=[pl.BlockSpec(memory_space=pltpu.SMEM)]
        + [pl.BlockSpec(memory_space=pl.ANY)] * len(pieces)
        + [
            pl.BlockSpec(near.shape, lambda i: (0, 0, 0)),
            pl.BlockSpec(side.shape, lambda i: (0, 0, 0)),
            pl.BlockSpec((VOCAB_TILE, D), lambda i: (i, 0)),
        ],
        out_specs=(
            pl.BlockSpec((4, slots), lambda i: (0, 0)),
            pl.BlockSpec((8, slots), lambda i: (0, 0)),
        ),
        scratch_shapes=[
            pltpu.VMEM((total, WIDE), jnp.bfloat16),
            pltpu.VMEM((5, total, 128), jnp.float32),
            pltpu.VMEM((5, slots, 128), jnp.float32),
            pltpu.SemaphoreType.DMA((len(pieces),)),
        ],
        compiler_params=score_params(),
        cost_estimate=score_cost(total, vocab_rows),
    )(place, *pieces, near, side, head_weight)


def finish_kernel(me_ref, gathered, info, device, offsets, lengths, logprob, entropy, sequence):
    peaks = gathered[:, 0, :]
    sums = gathered[:, 1, :]
    top = jnp.max(peaks, axis=0, keepdims=True)
    shift_by = peaks - top
    factor = jnp.exp(shift_by)
    sum_exp = jnp.sum(factor * sums, axis=0, keepdims=True)
    spread = jnp.sum(factor * (gathered[:, 2, :] + shift_by * sums), axis=0, keepdims=True)
    target_logit = jnp.sum(gathered[:, 3, :], axis=0, keepdims=True)
    log_total = jnp.log(sum_exp)
    valid = info[5:6, :] > 0.5
    row_logprob = jnp.where(valid, target_logit - top - log_total, 0.0)
    row_entropy = jnp.where(valid, log_total - spread / sum_exp, 0.0)
    position = device[...] * ROWS + info[4:5, :].astype(jnp.int32)
    position = jnp.where(valid, position, -1)
    own = me_ref[0] * ROWS + lax.broadcasted_iota(jnp.int32, (ROWS, 1), 0)
    mine = position == own

    def across(column):
        count = column.shape[0]
        row = lax.broadcasted_iota(jnp.int32, (count, count), 0)
        lane = lax.broadcasted_iota(jnp.int32, (count, count), 1)
        return jnp.sum(jnp.where(row == lane, column, 0), axis=0, keepdims=True)

    def down(line):
        count = line.shape[1]
        row = lax.broadcasted_iota(jnp.int32, (count, count), 0)
        lane = lax.broadcasted_iota(jnp.int32, (count, count), 1)
        return jnp.sum(jnp.where(row == lane, line, 0), axis=1, keepdims=True)

    logprob[...] = across(jnp.sum(jnp.where(mine, row_logprob, 0.0), axis=1, keepdims=True))
    entropy[...] = across(jnp.sum(jnp.where(mine, row_entropy, 0.0), axis=1, keepdims=True))
    first = down(offsets[...])
    inside = (position >= first) & (position < first + down(lengths[...]))
    totals = jnp.sum(jnp.where(inside, row_logprob, 0.0), axis=1, keepdims=True)
    sequence[...] = across(totals) / lengths[...].astype(jnp.float32)


def finish(me, gathered, info, offsets, lengths):
    vmem = pl.BlockSpec(memory_space=pltpu.VMEM)
    count = lengths.shape[0]
    return pl.pallas_call(
        finish_kernel,
        name="finish",
        compiler_params=pltpu.CompilerParams(vmem_limit_bytes=16 * 1024 * 1024),
        out_shape=(
            jax.ShapeDtypeStruct((1, ROWS), jnp.float32),
            jax.ShapeDtypeStruct((1, ROWS), jnp.float32),
            jax.ShapeDtypeStruct((1, count), jnp.float32),
        ),
        in_specs=[pl.BlockSpec(memory_space=pltpu.SMEM)] + [vmem] * 5,
        out_specs=(vmem, vmem, vmem),
    )(me[None], gathered, info, slot_devices()[None, :], offsets[None, :], lengths[None, :])


def slot_devices():
    device = np.zeros((64 * LIVE,), np.int32)
    for z in range(4):
        for y in range(4):
            for slot in range(LINE):
                at = (
                    z * 4 * ROWS_A + y * ROWS_A + slot
                    if slot < ROWS_A
                    else 16 * ROWS_A + y * 4 * ROWS_B + z * ROWS_B + slot - ROWS_A
                )
                device[at] = (slot // LIVE) * 16 + z * 4 + y
    return device


def local(hidden, norm_gain, head_weight, targets, lengths, offsets, loss_mask):
    me = lax.axis_index("tensor")
    x, z, y = me // 16, (me // 4) % 4, me % 4
    rows = pack(hidden, targets[None, :], loss_mask[None, :])
    line = [rows] + three_ahead(rows, X)
    part_a, part_b = prepare(x[None], norm_gain[None, :], line[:1] + [in_vmem(item) for item in line[1:]])
    row_a = [part_a] + three_ahead(part_a, Y)
    row_b = [part_b] + three_ahead(part_b, Z)
    own_a = jnp.concatenate(row_a, axis=0)
    own_b = jnp.concatenate(row_b, axis=0)
    up_a = from_ahead(own_a, Z, 1)
    down_a = from_ahead(own_a, Z, 3)
    up_b = from_ahead(own_b, Y, 1)
    down_b = from_ahead(own_b, Y, 3)
    na, nb = own_a.shape[0], own_b.shape[0]
    far_a = [from_ahead(up_a[: na // 2], Z, 1), from_ahead(down_a[na // 2 :], Z, 3)]
    far_a = [in_vmem(item) for item in far_a]
    far_b = [from_ahead(up_b[: nb // 2], Y, 1), from_ahead(down_b[nb // 2 :], Y, 3)]
    far_b = [in_vmem(item) for item in far_b]

    place = jnp.stack([me * head_weight.shape[0], z, y])
    held_weight = hold(head_weight)
    near = score_part(place, [own_a, own_b], held_weight)
    side = score_part(place, [up_a, down_a], held_weight)
    stats, info = score_rest(
        place, [*far_a, in_vmem(up_b), *far_b, in_vmem(down_b)], near, side, held_weight, na, nb
    )
    copies = jnp.broadcast_to(stats[None], (64,) + stats.shape)
    gathered = lax.all_to_all(copies, "tensor", 0, 0, tiled=True)
    token_logprob, token_entropy, score = finish(me, gathered, info, offsets, lengths)
    return token_logprob[0], token_entropy[0], score[0]


def solution(mesh):
    return jax.shard_map(
        local,
        mesh=mesh,
        in_specs=(
            P(("dp", "tensor"), None),
            P(),
            P(("dp", "tensor"), None),
            P(("dp", "tensor")),
            P("dp"),
            P("dp"),
            P(("dp", "tensor")),
        ),
        out_specs=(P(("dp", "tensor")), P(("dp", "tensor")), P("dp")),
        check_vma=False,
    )
```

```python
import functools

import jax
import jax.numpy as jnp
import numpy as np
from jax import lax
from jax.experimental import pallas as pl
from jax.experimental.pallas import tpu as pltpu
from jax.sharding import PartitionSpec as P


epsilon = 1e-05

D = 4096
WIDE = D + 128
ROWS = 16
LIVE = 10
LINE = 4 * LIVE
ROWS_A = 24
ROWS_B = LINE - ROWS_A
VOCAB_TILE = 1024


X, Z, Y = 0, 1, 2


def shifted_pairs(axis, step):
    pairs = []
    for index in range(64):
        coords = [index // 16, (index // 4) % 4, index % 4]
        coords[axis] = (coords[axis] - step) % 4
        pairs.append((index, coords[0] * 16 + coords[1] * 4 + coords[2]))
    return pairs


def from_ahead(value, axis, step):
    return lax.ppermute(value, "tensor", shifted_pairs(axis, step))


def three_ahead(value, axis):
    return [from_ahead(value, axis, 1), from_ahead(value, axis, 2), from_ahead(value, axis, 3)]


def in_vmem(value):
    return pltpu.with_memory_space_constraint(value, pltpu.VMEM)


def in_hbm(value):
    return pltpu.with_memory_space_constraint(value, pltpu.HBM)


def pack_kernel(hidden_ref, targets_ref, mask_ref, out_ref):
    row = lax.broadcasted_iota(jnp.int32, (ROWS, ROWS), 0)
    other = lax.broadcasted_iota(jnp.int32, (ROWS, ROWS), 1)

    def total(chosen, values):
        return jnp.sum(jnp.where(chosen, values, 0), axis=1, keepdims=True)

    target = total(row == other, targets_ref[...])
    columns = [
        total(other < row, mask_ref[...]),
        target >> 12,
        (target >> 6) & 63,
        target & 63,
        row[:, 0:1],
        total(row == other, mask_ref[...]),
    ]
    lane = lax.broadcasted_iota(jnp.int32, (ROWS, 128), 1)
    extra = jnp.zeros((ROWS, 128), jnp.int32)
    for k, column in enumerate(columns):
        extra = jnp.where(lane == k, column, extra)
    out_ref[:, :D] = hidden_ref[...]
    out_ref[:, D:] = extra.astype(jnp.float32).astype(jnp.bfloat16)


def pack(hidden, targets, mask):
    vmem = pl.BlockSpec(memory_space=pltpu.VMEM)
    return pl.pallas_call(
        pack_kernel,
        name="pack",
        out_shape=jax.ShapeDtypeStruct((ROWS, WIDE), jnp.bfloat16),
        in_specs=[vmem] * 3,
        out_specs=vmem,
        cost_estimate=pl.CostEstimate(
            flops=ROWS * WIDE, bytes_accessed=4 * ROWS * WIDE, transcendentals=0
        ),
    )(hidden, targets, mask)


def hold_kernel(weight_ref, out_ref, sem):
    copy = pltpu.make_async_copy(weight_ref, out_ref, sem)
    copy.start()
    copy.wait()


def hold(head_weight):
    return pl.pallas_call(
        hold_kernel,
        name="hold",
        out_shape=pltpu.VMEM(head_weight.shape, head_weight.dtype),
        in_specs=[pl.BlockSpec(memory_space=pl.ANY)],
        out_specs=pl.BlockSpec(memory_space=pltpu.VMEM),
        scratch_shapes=[pltpu.SemaphoreType.DMA],
        compiler_params=pltpu.CompilerParams(vmem_limit_bytes=4 * 1024 * 1024),
        cost_estimate=pl.CostEstimate(
            flops=0, bytes_accessed=2 * head_weight.size, transcendentals=0
        ),
    )(in_hbm(head_weight))


def prepare_kernel(own_ref, gain_ref, rows0, rows1, rows2, rows3, a_ref, b_ref):
    own = own_ref[0]
    normed, hots = [], []
    for k, ref in enumerate((rows0, rows1, rows2, rows3)):
        values = ref[:, :D].astype(jnp.float32)
        meansq = jnp.mean(values * values, axis=1, keepdims=True)
        scaled = values * lax.rsqrt(meansq + epsilon) * gain_ref[...]
        extra = ref[:, D:]
        normed.append(jnp.concatenate([scaled.astype(jnp.bfloat16), extra], axis=1))
        base = lax.rem(own + k, 4) * LIVE
        slot = extra[:, 0:1].astype(jnp.float32) + base.astype(jnp.float32)
        lane = lax.broadcasted_iota(jnp.int32, (ROWS, LINE), 1).astype(jnp.float32)
        live = extra[:, 5:6].astype(jnp.float32) > 0.5
        hots.append(jnp.where((slot == lane) & live, 1.0, 0.0).astype(jnp.bfloat16))
    hot = jnp.concatenate(hots, axis=0)
    rows = jnp.concatenate(normed, axis=0)
    line = lax.dot_general(
        hot, rows, (((0,), (0,)), ((), ())), preferred_element_type=jnp.float32
    ).astype(jnp.bfloat16)
    a_ref[...] = line[:ROWS_A]
    b_ref[...] = line[ROWS_A:]


def prepare(own, gain, pieces):
    vmem = pl.BlockSpec(memory_space=pltpu.VMEM)
    return pl.pallas_call(
        prepare_kernel,
        name="prepare",
        out_shape=(
            jax.ShapeDtypeStruct((ROWS_A, WIDE), jnp.bfloat16),
            jax.ShapeDtypeStruct((ROWS_B, WIDE), jnp.bfloat16),
        ),
        in_specs=[pl.BlockSpec(memory_space=pltpu.SMEM)] + [vmem] * 5,
        out_specs=(vmem, vmem),
        compiler_params=pltpu.CompilerParams(vmem_limit_bytes=8 * 1024 * 1024),
        cost_estimate=pl.CostEstimate(
            flops=2 * 64 * LINE * WIDE, bytes_accessed=104 * WIDE * 2, transcendentals=64
        ),
    )(own, gain, *pieces)


def join_kernel(*refs):
    out_ref, at = refs[-1], 0
    for ref in refs[:-1]:
        out_ref[at : at + ref.shape[0], :] = ref[...]
        at += ref.shape[0]


def join(pieces):
    vmem = pl.BlockSpec(memory_space=pltpu.VMEM)
    rows = sum(piece.shape[0] for piece in pieces)
    return pl.pallas_call(
        join_kernel,
        name="join",
        out_shape=jax.ShapeDtypeStruct((rows, WIDE), jnp.bfloat16),
        in_specs=[vmem] * len(pieces),
        out_specs=vmem,
        compiler_params=pltpu.CompilerParams(vmem_limit_bytes=4 * 1024 * 1024),
        cost_estimate=pl.CostEstimate(
            flops=rows * WIDE, bytes_accessed=4 * rows * WIDE, transcendentals=0
        ),
    )(*[in_vmem(piece) for piece in pieces])


def fetch(piece_refs, held, sems):
    copies, at = [], 0
    for k, ref in enumerate(piece_refs):
        rows = ref.shape[0]
        copies.append(pltpu.make_async_copy(ref, held.at[pl.ds(at, rows), :], sems.at[k]))
        at += rows
    for copy in copies:
        copy.start()
    for copy in copies:
        copy.wait()


def accumulate(step, vocab_rows, start, held, weight_ref, acc):
    rows = held.shape[0]

    @pl.when(step == 0)
    def _():
        acc[0] = jnp.full((rows, 128), -1e30, jnp.float32)
        acc[1] = jnp.zeros((rows, 128), jnp.float32)
        acc[2] = jnp.zeros((rows, 128), jnp.float32)
        acc[3] = jnp.zeros((rows, 128), jnp.float32)
        acc[4] = held[:, D:].astype(jnp.float32)

    tile = weight_ref.shape[0]
    scores = lax.dot_general(
        held[:, :D],
        weight_ref[...],
        (((1,), (1,)), ((), ())),
        preferred_element_type=jnp.float32,
    )
    lane = lax.broadcasted_iota(jnp.int32, (1, 128), 1)
    base = step * tile
    groups = [
        jnp.where(base + k + lane < vocab_rows, scores[:, k : k + 128], -1e30)
        for k in range(0, tile, 128)
    ]
    extra = acc[4]
    ids = extra[:, 1:2] * 4096.0 + extra[:, 2:3] * 64.0 + extra[:, 3:4]
    local_id = ids.astype(jnp.int32) - start
    local_id = jnp.where(local_id < vocab_rows, local_id, -1) - base
    before, sum_before = acc[0], acc[1]
    peak = functools.reduce(jnp.maximum, groups, before)
    shift_by = before - peak
    factor = jnp.exp(shift_by)
    total = factor * sum_before
    spread = factor * (acc[2] + shift_by * sum_before)
    picked = acc[3]
    for k, group in enumerate(groups):
        centred = group - peak
        expo = jnp.exp(centred)
        total = total + expo
        spread = spread + expo * centred
        picked = jnp.where(local_id == lane + 128 * k, group, picked)
    acc[0], acc[1], acc[2], acc[3] = peak, total, spread, picked


def near_kernel(vocab_rows, n_pieces, place_ref, *refs):
    weight_ref, acc, held, sems = refs[n_pieces:]
    step = pl.program_id(0)

    @pl.when(step == 0)
    def _():
        fetch(refs[:n_pieces], held, sems)

    accumulate(step, vocab_rows, place_ref[0], held, weight_ref, acc)


def rest_kernel(vocab_rows, n_pieces, na, nb, place_ref, *refs):
    near_ref, side_ref, weight_ref, out_ref, info_ref, held, acc, all_rows, sems = refs[n_pieces:]
    step = pl.program_id(0)

    @pl.when(step == 0)
    def _():
        fetch(refs[:n_pieces], held, sems)

    accumulate(step, vocab_rows, place_ref[0], held, weight_ref, acc)

    @pl.when(step == pl.num_programs(0) - 1)
    def _():
        z, y = place_ref[1], place_ref[2]
        for k in range(4):
            from_a, at_a = ((near_ref, 0), (side_ref, 0), (acc, 0), (side_ref, na))[k]
            from_b, at_b = (near_ref, na) if k == 0 else (acc, na + (k - 1) * nb)
            for j in range(4):
                to_a = lax.rem(z + k, 4) * na + lax.rem(y + j, 4) * ROWS_A
                to_b = 4 * na + lax.rem(y + k, 4) * nb + lax.rem(z + j, 4) * ROWS_B
                one_a = slice(at_a + j * ROWS_A, at_a + (j + 1) * ROWS_A)
                one_b = slice(at_b + j * ROWS_B, at_b + (j + 1) * ROWS_B)
                into_a = pl.ds(pl.multiple_of(to_a, 8), ROWS_A)
                into_b = pl.ds(pl.multiple_of(to_b, 8), ROWS_B)
                all_rows[:, into_a, :] = from_a[:, one_a, :]
                all_rows[:, into_b, :] = from_b[:, one_b, :]
        for at in range(0, all_rows.shape[1], 128):
            peaks, sums, spreads, picks, extra = [
                all_rows[plane, at : at + 128, :].T for plane in range(5)
            ]
            top = jnp.max(peaks, axis=0, keepdims=True)
            shift_by = peaks - top
            factor = jnp.exp(shift_by)
            here = slice(at, at + 128)
            out_ref[0:1, here] = top
            out_ref[1:2, here] = jnp.sum(factor * sums, axis=0, keepdims=True)
            out_ref[2:3, here] = jnp.sum(
                factor * (spreads + shift_by * sums), axis=0, keepdims=True
            )
            out_ref[3:4, here] = jnp.sum(picks, axis=0, keepdims=True)
            info_ref[:, here] = extra[:8]


def score_params():
    return pltpu.CompilerParams(vmem_limit_bytes=24 * 1024 * 1024)


def score_cost(total, vocab_rows):
    return pl.CostEstimate(
        flops=2 * total * vocab_rows * D,
        bytes_accessed=vocab_rows * D * 2 + total * WIDE * 2,
        transcendentals=total * vocab_rows,
    )


def score_part(place, pieces, head_weight):
    total = sum(piece.shape[0] for piece in pieces)
    vocab_rows = head_weight.shape[0]
    return pl.pallas_call(
        functools.partial(near_kernel, vocab_rows, len(pieces)),
        grid=(pl.cdiv(vocab_rows, VOCAB_TILE),),
        out_shape=jax.ShapeDtypeStruct((5, total, 128), jnp.float32),
        in_specs=[pl.BlockSpec(memory_space=pltpu.SMEM)]
        + [pl.BlockSpec(memory_space=pl.ANY)] * len(pieces)
        + [pl.BlockSpec((VOCAB_TILE, D), lambda i: (i, 0))],
        out_specs=pl.BlockSpec((5, total, 128), lambda i: (0, 0, 0)),
        scratch_shapes=[
            pltpu.VMEM((total, WIDE), jnp.bfloat16),
            pltpu.SemaphoreType.DMA((len(pieces),)),
        ],
        compiler_params=score_params(),
        cost_estimate=score_cost(total, vocab_rows),
    )(place, *pieces, head_weight)


def score_rest(place, pieces, near, side, head_weight, na, nb):
    total = sum(piece.shape[0] for piece in pieces)
    slots = 4 * (na + nb)
    vocab_rows = head_weight.shape[0]
    return pl.pallas_call(
        functools.partial(rest_kernel, vocab_rows, len(pieces), na, nb),
        name="rest",
        grid=(pl.cdiv(vocab_rows, VOCAB_TILE),),
        out_shape=(
            jax.ShapeDtypeStruct((4, slots), jnp.float32),
            jax.ShapeDtypeStruct((8, slots), jnp.float32),
        ),
        in_specs=[pl.BlockSpec(memory_space=pltpu.SMEM)]
        + [pl.BlockSpec(memory_space=pltpu.VMEM)] * len(pieces)
        + [
            pl.BlockSpec(near.shape, lambda i: (0, 0, 0)),
            pl.BlockSpec(side.shape, lambda i: (0, 0, 0)),
            pl.BlockSpec((VOCAB_TILE, D), lambda i: (i, 0)),
        ],
        out_specs=(
            pl.BlockSpec((4, slots), lambda i: (0, 0)),
            pl.BlockSpec((8, slots), lambda i: (0, 0)),
        ),
        scratch_shapes=[
            pltpu.VMEM((total, WIDE), jnp.bfloat16),
            pltpu.VMEM((5, total, 128), jnp.float32),
            pltpu.VMEM((5, slots, 128), jnp.float32),
            pltpu.SemaphoreType.DMA((len(pieces),)),
        ],
        compiler_params=score_params(),
        cost_estimate=score_cost(total, vocab_rows),
    )(place, *pieces, near, side, head_weight)


def finish_kernel(me_ref, gathered, info, device, offsets, lengths, logprob, entropy, sequence):
    peaks = gathered[:, 0, :]
    sums = gathered[:, 1, :]
    top = jnp.max(peaks, axis=0, keepdims=True)
    shift_by = peaks - top
    factor = jnp.exp(shift_by)
    sum_exp = jnp.sum(factor * sums, axis=0, keepdims=True)
    spread = jnp.sum(factor * (gathered[:, 2, :] + shift_by * sums), axis=0, keepdims=True)
    target_logit = jnp.sum(gathered[:, 3, :], axis=0, keepdims=True)
    log_total = jnp.log(sum_exp)
    valid = info[5:6, :] > 0.5
    row_logprob = jnp.where(valid, target_logit - top - log_total, 0.0)
    row_entropy = jnp.where(valid, log_total - spread / sum_exp, 0.0)
    position = device[...] * ROWS + info[4:5, :].astype(jnp.int32)
    position = jnp.where(valid, position, -1)
    own = me_ref[0] * ROWS + lax.broadcasted_iota(jnp.int32, (ROWS, 1), 0)
    mine = position == own

    def across(column):
        count = column.shape[0]
        row = lax.broadcasted_iota(jnp.int32, (count, count), 0)
        lane = lax.broadcasted_iota(jnp.int32, (count, count), 1)
        return jnp.sum(jnp.where(row == lane, column, 0), axis=0, keepdims=True)

    def down(line):
        count = line.shape[1]
        row = lax.broadcasted_iota(jnp.int32, (count, count), 0)
        lane = lax.broadcasted_iota(jnp.int32, (count, count), 1)
        return jnp.sum(jnp.where(row == lane, line, 0), axis=1, keepdims=True)

    logprob[...] = across(jnp.sum(jnp.where(mine, row_logprob, 0.0), axis=1, keepdims=True))
    entropy[...] = across(jnp.sum(jnp.where(mine, row_entropy, 0.0), axis=1, keepdims=True))
    first = down(offsets[...])
    inside = (position >= first) & (position < first + down(lengths[...]))
    totals = jnp.sum(jnp.where(inside, row_logprob, 0.0), axis=1, keepdims=True)
    sequence[...] = across(totals) / lengths[...].astype(jnp.float32)


def finish(me, gathered, info, offsets, lengths):
    vmem = pl.BlockSpec(memory_space=pltpu.VMEM)
    count = lengths.shape[0]
    return pl.pallas_call(
        finish_kernel,
        name="finish",
        compiler_params=pltpu.CompilerParams(vmem_limit_bytes=16 * 1024 * 1024),
        out_shape=(
            jax.ShapeDtypeStruct((1, ROWS), jnp.float32),
            jax.ShapeDtypeStruct((1, ROWS), jnp.float32),
            jax.ShapeDtypeStruct((1, count), jnp.float32),
        ),
        in_specs=[pl.BlockSpec(memory_space=pltpu.SMEM)] + [vmem] * 5,
        out_specs=(vmem, vmem, vmem),
    )(me[None], gathered, info, slot_devices()[None, :], offsets[None, :], lengths[None, :])


def slot_devices():
    device = np.zeros((64 * LIVE,), np.int32)
    for z in range(4):
        for y in range(4):
            for slot in range(LINE):
                at = (
                    z * 4 * ROWS_A + y * ROWS_A + slot
                    if slot < ROWS_A
                    else 16 * ROWS_A + y * 4 * ROWS_B + z * ROWS_B + slot - ROWS_A
                )
                device[at] = (slot // LIVE) * 16 + z * 4 + y
    return device


def local(hidden, norm_gain, head_weight, targets, lengths, offsets, loss_mask):
    me = lax.axis_index("tensor")
    x, z, y = me // 16, (me // 4) % 4, me % 4
    rows = pack(hidden, targets[None, :], loss_mask[None, :])
    line = [rows] + three_ahead(rows, X)
    part_a, part_b = prepare(
        x[None], in_hbm(norm_gain[None, :]), [in_hbm(rows)] + [in_vmem(item) for item in line[1:]]
    )
    row_a = [part_a] + three_ahead(part_a, Y)
    row_b = [part_b] + three_ahead(part_b, Z)
    own_a = jnp.concatenate(row_a, axis=0)
    own_b = join(row_b)
    up_a = from_ahead(own_a, Z, 1)
    down_a = from_ahead(own_a, Z, 3)
    up_b = from_ahead(own_b, Y, 1)
    down_b = from_ahead(own_b, Y, 3)
    na, nb = own_a.shape[0], own_b.shape[0]
    far_a = [from_ahead(up_a[: na // 2], Z, 1), from_ahead(down_a[na // 2 :], Z, 3)]
    far_a = [in_vmem(item) for item in far_a]
    far_b = [from_ahead(up_b[: nb // 2], Y, 1), from_ahead(down_b[nb // 2 :], Y, 3)]
    far_b = [in_vmem(item) for item in far_b]

    place = jnp.stack([me * head_weight.shape[0], z, y])
    held_weight = hold(head_weight)
    near = score_part(place, [in_vmem(own_a), in_vmem(own_b)], held_weight)
    side = score_part(place, [up_a, down_a], held_weight)
    stats, info = score_rest(
        place, [*far_a, in_vmem(up_b), *far_b, in_vmem(down_b)], near, side, held_weight, na, nb
    )
    copies = jnp.broadcast_to(stats[None], (64,) + stats.shape)
    gathered = lax.all_to_all(copies, "tensor", 0, 0, tiled=True)
    token_logprob, token_entropy, score = finish(me, gathered, info, offsets, lengths)
    return token_logprob[0], token_entropy[0], score[0]


def solution(mesh):
    return jax.shard_map(
        local,
        mesh=mesh,
        in_specs=(
            P(("dp", "tensor"), None),
            P(),
            P(("dp", "tensor"), None),
            P(("dp", "tensor")),
            P("dp"),
            P("dp"),
            P(("dp", "tensor")),
        ),
        out_specs=(P(("dp", "tensor")), P(("dp", "tensor")), P("dp")),
        check_vma=False,
    )
```
